512 devices in a mesh: dp: 8 (over y), expert: 64 (over x, z, core).
Axes of the slice: x: 4, y: 8, z: 8, core: 2. Of those that a mesh axis runs over, the one named last changes fastest.
Arguments:
- tokens: bfloat16 [65536, 2048], P(('dp', 'expert')), may hold values from -6 to 6
- cotangent: bfloat16 [65536, 2048], P(('dp', 'expert')), may hold values from -6 to 6
- routes: int32 [65536, 2], P(('dp', 'expert')), may hold values from 0 to 63, all different within a row; in each aligned block of 128 rows (0 to 127, 128 to 255, ...) at most 6 rows name the same one
- gates: float32 [65536, 2], P(('dp', 'expert')), may hold values from 0.1 to 1
- w_gate: bfloat16 [64, 2048, 768], P('expert', None, 'dp'), may hold values from -0.125 to 0.125
- w_up: bfloat16 [64, 2048, 768], P('expert', None, 'dp'), may hold values from -0.125 to 0.125
- w_down: bfloat16 [64, 768, 2048], P('expert', 'dp'), may hold values from -0.21875 to 0.21875
Outputs:
- mixed: bfloat16 [65536, 2048], P(('dp', 'expert'))
- token_grad: bfloat16 [65536, 2048], P(('dp', 'expert'))
- gate_grad: float32 [65536, 2], P(('dp', 'expert'))
The draws below stay inside these ranges and needn't reach their ends.
Inputs may be any that keep to these rules, and one draw needn't show every extreme that they name: `routes`: each row names 2 different experts. In each aligned block of 128 rows (the rows of one device), no expert is named by more than 6 rows, a bound that some block reaches.
All inputs are finite; a program needn't handle non-finite values.
Results may differ from the reference program's by a relative error of at most 0.014.
Values may be sent and summed in bfloat16 or wider, within the bound.
A program may use at most 64 MiB of HBM per device.

```python
import math
import jax
import jax.numpy as jnp
import numpy as np
from jax import lax

D = 2048
FF = 768
TOP = 2
TOK_DEV = 128
EXPERTS = 64
CAP = 6
TOKENS = 65536
N_DP = 8
N_EXPERT = 64


def level_of(own_key, dims, cuts, low, largest):
    gain, own = 1.0, jax.random.fold_in(own_key, 6)
    for axis_at, blocks in cuts:
        steps = jnp.exp(jax.random.uniform(jax.random.fold_in(own, axis_at), (blocks,), jnp.float32, low / len(cuts), largest / len(cuts)))
        gain = gain * jnp.repeat(steps, dims[axis_at] // blocks).reshape([-1 if axis == axis_at else 1 for axis in range(len(dims))])
    return gain


def routed_block(rng, own, number, rows, amount, top, most, slope):
    order = jax.random.permutation(rng, amount)
    crowded, common = shares(amount, rows * top, most, slope, True), shares(amount, rows * top, most, slope, False)
    places = jnp.arange(amount)

    def named(lengths, rotation):
        used = int((lengths > 0).sum())
        fixed = max(1, used // 4)
        passed = fixed + (places - fixed + rotation * (used - fixed)) % max(1, amount - fixed)
        return jnp.zeros((amount,), jnp.int32).at[order[jnp.where(places < fixed, places, passed)]].set(jnp.asarray(lengths, jnp.int32))

    lengths = jnp.where(number % 4 == 0, named(crowded, number // 4), named(common, number - number // 4 - 1))
    mixed = jax.random.permutation(jax.random.fold_in(own, 3), amount)
    source_of, taker = mixed[0:amount // 2 * 2:2], mixed[1:amount // 2 * 2:2]
    margin = jnp.minimum(lengths[source_of] - 1, most - lengths[taker]) // 2
    margin = jnp.where((source_of == order[0]) | (taker == order[0]) | (lengths[taker] == 0), 0, jnp.maximum(margin, 0))
    passed = jax.random.randint(jax.random.fold_in(own, 4), (amount // 2,), 0, 1 << 20) % (margin + 1)
    lengths = lengths.at[source_of].add(-passed).at[taker].add(passed)
    items = jnp.searchsorted(jnp.cumsum(lengths), jnp.arange(rows * top), side="right").astype(jnp.int32)
    grid = items.reshape(top, rows).T
    grid = grid[jax.random.permutation(jax.random.fold_in(own, 1), rows)]
    rotation = jax.random.randint(jax.random.fold_in(own, 2), (rows, 1), 0, top)
    return jnp.take_along_axis(grid, (jnp.arange(top)[None, :] + rotation) % top, axis=1)


def shares(number_of, total, most, slope, full):
    loads = [(1 << 20) // math.isqrt(standing ** slope) + 1 for standing in range(1, number_of + 1)]
    largest = most if full else min(most, max(-(-total // number_of), total * loads[0] // sum(loads)))
    least = 1 if total - largest >= number_of - 1 else 0
    given, surplus = [largest] + [least] * (number_of - 1), total - largest - least * (number_of - 1)
    while surplus > 0:
        candidates = [i for i in range(1, number_of) if given[i] < largest] or [i for i in range(1, number_of) if given[i] < most]
        mass, remaining = sum([loads[i] for i in candidates]), surplus
        for i in candidates:
            addition = min(most - given[i], max(1, remaining * loads[i] // mass), surplus)
            given[i] = given[i] + addition
            surplus = surplus - addition
    return np.array(given)


def noise(key, dims, spread, most, split=(), held_as=jnp.bfloat16):
    array = jax.random.normal(key, dims, jnp.float32) * spread
    if len(split) > 0:
        array = level_of(key, dims, split, -0.22, 0.18) * array
    return jnp.clip(array, min=-most, max=most).astype(held_as)


def setup_inputs(seed: int = 0) -> dict:
    key_of = jax.random.split(jax.random.key(seed), 8)
    tokens = noise(key_of[0], (TOKENS, D), 1.0, 6.0, ((0, 512),))
    cotangent = noise(key_of[1], (TOKENS, D), 1.0, 6.0, ((0, 512),))
    routes_keys = jax.random.split(jax.random.fold_in(key_of[2], 1), TOKENS // TOK_DEV)
    routes_turns = jax.random.permutation(jax.random.fold_in(key_of[2], 3), TOKENS // TOK_DEV)
    routes = jax.vmap(lambda own, number: routed_block(jax.random.fold_in(key_of[2], 2), own, number, TOK_DEV, EXPERTS, TOP, CAP, 2))(routes_keys, routes_turns).reshape((TOKENS, TOP))
    gates = jnp.clip(jnp.exp(math.log(1.0) - 2.3025851 * jax.random.uniform(key_of[3], (TOKENS, TOP), jnp.float32) ** level_of(key_of[3], (TOKENS, TOP), ((0, 512),), -0.2, 0.2)), 0.1, 1.0)
    w_gate = noise(key_of[4], (EXPERTS, D, FF), D ** -0.5, 0.125, ((0, 64), (2, 8)))
    w_up = noise(key_of[5], (EXPERTS, D, FF), D ** -0.5, 0.125, ((0, 64), (2, 8)))
    w_down = noise(key_of[6], (EXPERTS, FF, D), FF ** -0.5, 0.21875, ((0, 64), (1, 8)))
    return {"tokens": tokens, "cotangent": cotangent, "routes": routes, "gates": gates, "w_gate": w_gate, "w_up": w_up, "w_down": w_down}


def expert_rows(rows, back_rows, weight_rows, gate_w, up_w, down_w):
    pre_gate = jnp.dot(rows, gate_w, preferred_element_type=jnp.float32)
    pre_up = jnp.dot(rows, up_w, preferred_element_type=jnp.float32)
    sig = jax.nn.sigmoid(pre_gate)
    act = pre_gate * sig
    hidden = (act * pre_up).astype(jnp.bfloat16)
    raw_out = jnp.dot(hidden, down_w, preferred_element_type=jnp.float32)
    slot_out = (weight_rows[:, None] * raw_out).astype(jnp.bfloat16)
    back_hidden = jnp.dot(back_rows, down_w.T, preferred_element_type=jnp.float32)
    gate_part = jnp.sum(hidden.astype(jnp.float32) * back_hidden, axis=1)
    scaled = weight_rows[:, None] * back_hidden
    back_gate = (scaled * pre_up * sig * (1.0 + pre_gate * (1.0 - sig))).astype(jnp.bfloat16)
    back_up = (scaled * act).astype(jnp.bfloat16)
    slot_grad = jnp.dot(back_gate, gate_w.T, preferred_element_type=jnp.float32)
    slot_grad = (slot_grad + jnp.dot(back_up, up_w.T, preferred_element_type=jnp.float32)).astype(jnp.bfloat16)
    return slot_out, slot_grad, gate_part


def reference(tokens, cotangent, routes, gates, w_gate, w_up, w_down):
    slots = TOKENS * TOP
    most_rows = N_DP * N_EXPERT * CAP
    expert_ids = routes.reshape(slots).astype(jnp.int32)
    onehot = (expert_ids[:, None] == jnp.arange(EXPERTS, dtype=jnp.int32)[None, :]).astype(jnp.int32)
    slot_rank = jnp.sum(onehot * (jnp.cumsum(onehot, axis=0) - onehot), axis=1).astype(jnp.int32)
    table = jnp.full((EXPERTS * most_rows,), slots, jnp.int32)
    table = table.at[expert_ids * most_rows + slot_rank].set(jnp.arange(slots, dtype=jnp.int32))
    table = table.reshape(EXPERTS, most_rows)
    padded_tok = jnp.concatenate([tokens, jnp.zeros((1, D), jnp.bfloat16)], axis=0)
    padded_cot = jnp.concatenate([cotangent, jnp.zeros((1, D), jnp.bfloat16)], axis=0)
    padded_gate = jnp.concatenate([gates.reshape(slots), jnp.zeros((1,), jnp.float32)], axis=0)

    def one_expert(carry, item):
        out_acc, grad_acc, gate_acc = carry
        gate_w, up_w, down_w, row_table = item
        tok_index = jnp.where(row_table < slots, row_table // TOP, TOKENS).astype(jnp.int32)
        slot_out, slot_grad, gate_part = expert_rows(padded_tok[tok_index], padded_cot[tok_index],
                                                     padded_gate[row_table], gate_w, up_w, down_w)
        out_acc = out_acc.at[tok_index].add(slot_out.astype(jnp.float32))
        grad_acc = grad_acc.at[tok_index].add(slot_grad.astype(jnp.float32))
        gate_acc = gate_acc.at[row_table].add(gate_part)
        return (out_acc, grad_acc, gate_acc), None

    start = (jnp.zeros((TOKENS + 1, D), jnp.float32), jnp.zeros((TOKENS + 1, D), jnp.float32),
             jnp.zeros((slots + 1,), jnp.float32))
    (out_acc, grad_acc, gate_acc), _ = lax.scan(one_expert, start, (w_gate, w_up, w_down, table))
    mixed = out_acc[:TOKENS].astype(jnp.bfloat16)
    token_grad = grad_acc[:TOKENS].astype(jnp.bfloat16)
    gate_grad = gate_acc[:slots].reshape(TOKENS, TOP)
    return mixed, token_grad, gate_grad
```

```python
import functools

import jax
import jax.numpy as jnp
import numpy as np
from jax import lax
from jax.experimental import pallas as pl
from jax.experimental.pallas import tpu as pltpu
from jax.sharding import PartitionSpec as P

MESH = pl.DeviceIdType.MESH
CAP = 6
NC = 2
SIZES = {64: (4, 8)}
CHUNKS = 4
NT = (((1,), (1,)), ((), ()))


def log2(n):
    return n.bit_length() - 1


def kernel(
    nx, nz, ny,
    tok_ref, cot_ref, routes_ref, gates_ref, perm_ref, wg_ref, wu_ref, wd_ref,
    mixed_ref, grad_ref, gg_ref,
    pk, xr, zs, zr, w, pre_g, pre_u, hid, bg, bu, zo, zor, xo, xor, m0, m1,
    s_x, r_x, s_z, r_z, s_zo, r_zo, s_xo, r_xo, s_ring, r_ring, s_own, gate_sem,
):
    nk = nx * NC
    experts = nk * nz
    slots = experts * CAP
    tok, width = tok_ref.shape
    cw = width // CHUNKS
    fs = wg_ref.shape[0]
    half = fs // 2
    hops = ny // 2
    total = 2 * CHUNKS

    y = lax.axis_index("dp")
    e = lax.axis_index("expert")
    x, z, c = e // (nz * NC), (e // NC) % nz, e % NC

    def dev(dy, dx, dz, dc):
        return (
            lax.rem(y + dy + ny, ny),
            lax.rem(x + dx + nx, nx) * (nz * NC) + lax.rem(z + dz + nz, nz) * NC + lax.rem(c + dc, NC),
        )

    x_deltas = [(k // NC, k % NC) for k in range(nk)]
    to_x = [dev(0, dx, 0, dc) for dx, dc in x_deltas]
    from_x = [dev(0, -dx, 0, dc) for dx, dc in x_deltas]
    to_z = [dev(0, 0, dz, 0) for dz in range(nz)]
    from_z = [dev(0, 0, -dz, 0) for dz in range(nz)]
    ring_dev = (dev(1, 0, 0, 0), dev(-1, 0, 0, 0))
    partner = dev(0, 0, 0, 1)

    own = (hops - 1) * 2 * fs
    own_copies = [
        pltpu.make_async_copy(ref, w.at[i, pl.ds(own, fs), :], s_own.at[i])
        for i, ref in enumerate((wg_ref, wu_ref, wd_ref))
    ]
    for copy in own_copies:
        copy.start()

    barrier = pltpu.get_barrier_semaphore()
    peers = to_x[1:] + to_z[1:] + list(ring_dev)
    for d in peers:
        pl.semaphore_signal(barrier, inc=1, device_id=d, device_id_type=MESH)

    ids = [routes_ref[k : k + 1, :] for k in range(2)]
    expert_row = lax.broadcasted_iota(jnp.int32, (experts, tok), 0)
    hot = [(expert_row == i).astype(jnp.float32) for i in ids]
    earlier = (
        lax.broadcasted_iota(jnp.int32, (tok, tok), 0) < lax.broadcasted_iota(jnp.int32, (tok, tok), 1)
    ).astype(jnp.bfloat16)
    count = jnp.dot((hot[0] + hot[1]).astype(jnp.bfloat16), earlier, preferred_element_type=jnp.float32)
    slot_row = lax.broadcasted_iota(jnp.int32, (slots, tok), 0)
    hits = []
    for k in range(2):
        rank = jnp.sum(hot[k] * count, axis=0, keepdims=True).astype(jnp.int32)
        i = ids[k]
        dx = ((i >> log2(nz * NC)) - x) & (nx - 1)
        dz = (((i >> 1) & (nz - 1)) - z) & (nz - 1)
        dc = ((i & 1) - c) & 1
        slot = ((dx * NC + dc) * nz + dz) * CAP + rank
        hits.append((slot_row == slot).astype(jnp.float32))
    m0[...] = hits[0].T.astype(jnp.bfloat16)
    m1[...] = hits[1].T.astype(jnp.bfloat16)
    pack = (hits[0] + hits[1]).astype(jnp.bfloat16)

    pl.semaphore_wait(barrier, len(peers))

    def x_copy(n, k):
        return pltpu.make_async_remote_copy(
            src_ref=pk.at[n, k], dst_ref=xr.at[n, k], send_sem=s_x.at[n], recv_sem=r_x.at[n],
            device_id=to_x[k], device_id_type=MESH)

    def z_copy(n, dz):
        return pltpu.make_async_remote_copy(
            src_ref=zs.at[n, dz], dst_ref=zr.at[n, dz], send_sem=s_z.at[n], recv_sem=r_z.at[n],
            device_id=to_z[dz], device_id_type=MESH)

    def zo_copy(n, dz):
        return pltpu.make_async_remote_copy(
            src_ref=zo.at[n, dz], dst_ref=zor.at[n, dz], send_sem=s_zo.at[n], recv_sem=r_zo.at[n],
            device_id=from_z[dz], device_id_type=MESH)

    def xo_copy(n, k):
        return pltpu.make_async_remote_copy(
            src_ref=xo.at[n, k], dst_ref=xor.at[n, k], send_sem=s_xo.at[n], recv_sem=r_xo.at[n],
            device_id=from_x[k], device_id_type=MESH)

    def all_of(n, count_, src, dst, s_sem, r_sem):
        return pltpu.make_async_remote_copy(
            src_ref=src.at[n, pl.ds(1, count_ - 1)], dst_ref=dst.at[n, pl.ds(1, count_ - 1)],
            send_sem=s_sem.at[n], recv_sem=r_sem.at[n], device_id=partner, device_id_type=MESH)

    def x_all(n):
        return all_of(n, nk, pk, xr, s_x, r_x)

    def z_all(n):
        return all_of(n, nz, zs, zr, s_z, r_z)

    def zo_all(n):
        return all_of(n, nz, zo, zor, s_zo, r_zo)

    def xo_all(n):
        return all_of(n, nk, xo, xor, s_xo, r_xo)

    def dispatch(base, ref):
        def step(n, carry):
            cols = pl.ds(pl.multiple_of(n * cw, cw), cw)
            rows = jnp.dot(pack, ref[:, cols], preferred_element_type=jnp.float32).astype(jnp.bfloat16)
            rows = rows.reshape(nk, nz * CAP, cw)
            pk[base + n] = rows
            xr[base + n, 0] = rows[0]
            for k in range(1, nk):
                x_copy(base + n, k).start()
            return carry

        lax.fori_loop(0, CHUNKS, step, 0)

    pieces = 6

    def ring_row(direction, d, h):
        if isinstance(d, int) and d == 0:
            return own + h * half
        if isinstance(d, int) and d == hops:
            return own + fs + h * half
        return (d - 1) * 2 * fs + direction * fs + h * half

    def ring_copy(direction, d, i, h):
        src = pl.ds(ring_row(direction, d - 1, h), half)
        dst = pl.ds(ring_row(direction, d, h), half)
        at = i * 2 + h
        return pltpu.make_async_remote_copy(
            src_ref=w.at[i, src, :], dst_ref=w.at[i, dst, :],
            send_sem=s_ring.at[direction, d - 1, at], recv_sem=r_ring.at[direction, d - 1, at],
            device_id=ring_dev[direction], device_id_type=MESH)

    def goes(direction, d, h):
        return d < hops or h == direction

    def ring_start():
        for p in range(pieces):
            for direction in range(2):
                if goes(direction, 1, p % 2):
                    ring_copy(direction, 1, p // 2, p % 2).start()

    def ring_event(j):
        d, p = j // pieces + 1, j % pieces
        for direction in range(2):
            ring_copy(direction, d, p // 2, p % 2).wait_recv()
            if goes(direction, d + 1, p % 2):
                ring_copy(direction, d + 1, p // 2, p % 2).start()

    def ring_last():
        for i in range(3):
            for direction in range(2):
                ring_copy(direction, hops, i, direction).wait_recv()

    events = (hops - 1) * pieces

    def forward_chunk(n):
        x_all(n).wait_recv()
        rows = jnp.dot(perm_ref[...], xr[n].reshape(slots, cw), preferred_element_type=jnp.float32)
        rows = rows.astype(jnp.bfloat16).reshape(nz, nk * CAP, cw)
        zs[n] = rows
        zr[n, 0] = rows[0]
        for dz in range(1, nz):
            z_copy(n, dz).start()

    def wait_own():
        for copy in own_copies:
            copy.wait()

    wait_own()

    @pl.when(c == 0)
    def _():
        ring_start()

    dispatch(0, tok_ref)
    dispatch(CHUNKS, cot_ref)

    @pl.when(c == 0)
    def _():
        per = -(-events // total)
        for n in range(total):
            forward_chunk(n)
            for j in range(n * per, min(events, (n + 1) * per)):
                ring_event(j)
        ring_last()
        pl.semaphore_signal(gate_sem, inc=1, device_id=partner, device_id_type=MESH)

    @pl.when(c == 1)
    def _():
        def step(n, carry):
            forward_chunk(n)
            return carry

        lax.fori_loop(0, total, step, 0)
        pl.semaphore_wait(gate_sem, 1)
        ring_start()

    def wide(base):
        return jnp.concatenate([zr[base + n].reshape(slots, cw) for n in range(CHUNKS)], axis=1)

    for n in range(CHUNKS):
        z_all(n).wait_recv()
    for g in range(hops):
        @pl.when(c == 1)
        def _():
            if g < hops - 1:
                for j in range(g * pieces, (g + 1) * pieces):
                    ring_event(j)
            else:
                ring_last()

        span = pl.ds(g * 2 * fs, 2 * fs)
        rows = wide(0)
        gate = lax.dot_general(rows, w[0, span, :], NT, preferred_element_type=jnp.float32)
        up = lax.dot_general(rows, w[1, span, :], NT, preferred_element_type=jnp.float32)
        pre_g[g] = gate
        pre_u[g] = up
        hid[g] = (gate * jax.nn.sigmoid(gate) * up).astype(jnp.bfloat16)

    def ship(n, rows):
        rows = rows.astype(jnp.bfloat16).reshape(nz, nk * CAP, cw)
        zo[n] = rows
        zor[n, 0] = rows[0]
        for dz in range(1, nz):
            zo_copy(n, dz).start()

    def out_step(n, carry):
        cols = pl.ds(pl.multiple_of(n * cw, cw), cw)
        acc = jnp.zeros((slots, cw), jnp.float32)
        for g in range(hops):
            acc = acc + jnp.dot(
                hid[g], w[2, pl.ds(g * 2 * fs, 2 * fs), cols], preferred_element_type=jnp.float32)
        ship(n, acc)
        return carry

    lax.fori_loop(0, CHUNKS, out_step, 0)

    for n in range(CHUNKS):
        z_all(CHUNKS + n).wait_recv()

    def back_step(g, carry):
        span = pl.ds(pl.multiple_of(g * 2 * fs, 2 * fs), 2 * fs)
        back = lax.dot_general(wide(CHUNKS), w[2, span, :], NT, preferred_element_type=jnp.float32)
        gate, up = pre_g[g], pre_u[g]
        sig = jax.nn.sigmoid(gate)
        bg[g] = (back * up * sig * (1.0 + gate * (1.0 - sig))).astype(jnp.bfloat16)
        bu[g] = (back * (gate * sig)).astype(jnp.bfloat16)
        return carry

    lax.fori_loop(0, hops, back_step, 0)

    def grad_step(n, carry):
        cols = pl.ds(pl.multiple_of(n * cw, cw), cw)
        acc = jnp.zeros((slots, cw), jnp.float32)
        for g in range(hops):
            span = pl.ds(g * 2 * fs, 2 * fs)
            acc = acc + jnp.dot(bg[g], w[0, span, cols], preferred_element_type=jnp.float32)
            acc = acc + jnp.dot(bu[g], w[1, span, cols], preferred_element_type=jnp.float32)
        ship(CHUNKS + n, acc)
        return carry

    lax.fori_loop(0, CHUNKS, grad_step, 0)

    def back_chunk(n):
        zo_all(n).wait_recv()
        rows = jnp.dot(perm_ref[...], zor[n].reshape(slots, cw), preferred_element_type=jnp.float32)
        rows = rows.astype(jnp.bfloat16).reshape(nk, nz * CAP, cw)
        xo[n] = rows
        xor[n, 0] = rows[0]
        for k in range(1, nk):
            xo_copy(n, k).start()

    weight = [jnp.broadcast_to(gates_ref[k : k + 1, :], (tok, tok)).T[:, 0:1] for k in range(2)]

    def picked(n):
        xo_all(n).wait_recv()
        rows = xor[n].reshape(slots, cw)
        return (
            jnp.dot(m0[...], rows, preferred_element_type=jnp.float32),
            jnp.dot(m1[...], rows, preferred_element_type=jnp.float32),
        )

    def combine_out(n, sums):
        a, b = picked(n)
        cols = pl.ds(pl.multiple_of(n * cw, cw), cw)
        mixed_ref[:, cols] = (weight[0] * a + weight[1] * b).astype(jnp.bfloat16)
        cot = cot_ref[:, cols].astype(jnp.float32)
        return (
            sums[0] + jnp.sum(cot * a, axis=1, keepdims=True),
            sums[1] + jnp.sum(cot * b, axis=1, keepdims=True),
        )

    def combine_grad(n):
        a, b = picked(CHUNKS + n)
        cols = pl.ds(pl.multiple_of(n * cw, cw), cw)
        grad_ref[:, cols] = (weight[0] * a + weight[1] * b).astype(jnp.bfloat16)

    back_chunk(0)

    def out_loop(n, sums):
        back_chunk(n + 1)
        return combine_out(n, sums)

    sums = lax.fori_loop(
        0, CHUNKS, out_loop, (jnp.zeros((tok, 1), jnp.float32), jnp.zeros((tok, 1), jnp.float32)))
    for k in range(2):
        gg_ref[k : k + 1, :] = jnp.broadcast_to(sums[k], (tok, tok)).T[0:1, :]

    def grad_loop(n, carry):
        back_chunk(CHUNKS + n + 1)
        combine_grad(n)
        return carry

    lax.fori_loop(0, CHUNKS - 1, grad_loop, 0)
    combine_grad(CHUNKS - 1)

    def drain(n, carry):
        x_all(n).wait_send()
        z_all(n).wait_send()
        zo_all(n).wait_send()
        xo_all(n).wait_send()
        return carry

    lax.fori_loop(0, total, drain, 0)
    for d in range(1, hops + 1):
        for p in range(pieces):
            for direction in range(2):
                if goes(direction, d, p % 2):
                    ring_copy(direction, d, p // 2, p % 2).wait_send()


def body(tokens, cotangent, routes, gates, w_gate, w_up, w_down):
    tok, width = tokens.shape
    ny, ne = lax.axis_size("dp"), lax.axis_size("expert")
    nx, nz = SIZES[ne]
    nk = nx * NC
    fs = w_down.shape[1]
    slots = ne * CAP
    cw = width // CHUNKS
    total = 2 * CHUNKS
    hops = ny // 2
    assert nk == nz and fs % 2 == 0
    perm = np.zeros((slots, slots), np.float32)
    for a in range(nz):
        for b in range(nk):
            for r in range(CAP):
                perm[(a * nk + b) * CAP + r, (b * nz + a) * CAP + r] = 1.0
    vmem = pl.BlockSpec(memory_space=pltpu.VMEM)
    any_ = pl.BlockSpec(memory_space=pl.ANY)
    dma = pltpu.SemaphoreType.DMA
    blocks = pltpu.VMEM((total, nz, nk * CAP, cw), jnp.bfloat16)
    hidden = (hops, slots, 2 * fs)
    mixed, token_grad, gate_grad = pl.pallas_call(
        functools.partial(kernel, nx, nz, ny),
        out_shape=(
            jax.ShapeDtypeStruct((tok, width), jnp.bfloat16),
            jax.ShapeDtypeStruct((tok, width), jnp.bfloat16),
            jax.ShapeDtypeStruct((2, tok), jnp.float32),
        ),
        in_specs=[vmem, vmem, vmem, vmem, vmem, any_, any_, any_],
        out_specs=(vmem, vmem, vmem),
        scratch_shapes=[
            blocks, blocks, blocks, blocks,
            pltpu.VMEM((3, ny * fs, width), jnp.bfloat16),
            pltpu.VMEM(hidden, jnp.float32), pltpu.VMEM(hidden, jnp.float32),
            pltpu.VMEM(hidden, jnp.bfloat16), pltpu.VMEM(hidden, jnp.bfloat16), pltpu.VMEM(hidden, jnp.bfloat16),
            blocks, blocks, blocks, blocks,
            pltpu.VMEM((tok, slots), jnp.bfloat16), pltpu.VMEM((tok, slots), jnp.bfloat16),
            dma((total,)), dma((total,)), dma((total,)), dma((total,)),
            dma((total,)), dma((total,)), dma((total,)), dma((total,)),
            dma((2, hops, 6)), dma((2, hops, 6)), dma((3,)),
            pltpu.SemaphoreType.REGULAR,
        ],
        compiler_params=pltpu.CompilerParams(
            collective_id=0, has_side_effects=True, vmem_limit_bytes=63 * 1024 * 1024),
    )(
        tokens, cotangent, routes.T, gates.T, jnp.asarray(perm, jnp.bfloat16),
        jnp.swapaxes(w_gate, 1, 2)[0], jnp.swapaxes(w_up, 1, 2)[0], w_down[0],
    )
    return mixed, token_grad, gate_grad.T


def solution(mesh):
    return jax.shard_map(
        body,
        mesh=mesh,
        in_specs=(
            P(("dp", "expert"), None),
            P(("dp", "expert"), None),
            P(("dp", "expert"), None),
            P(("dp", "expert"), None),
            P("expert", None, "dp"),
            P("expert", None, "dp"),
            P("expert", "dp", None),
        ),
        out_specs=(P(("dp", "expert"), None), P(("dp", "expert"), None), P(("dp", "expert"), None)),
        check_vma=False,
    )
```
